256 devices in a mesh: gx: 8 (over y, core), gy: 32 (over x, z).
Axes of the slice: x: 4, y: 4, z: 8, core: 2. Of those that a mesh axis runs over, the one named last changes fastest.
Arguments:
- motion: float32 [768, 512, 3, 512], P('gx', 'gy'), may hold values from -40 to 40
- time_sketch: float32 [512, 128], replicated, may hold values from -0.25 to 0.25
- x_sketch: float32 [768, 128], replicated, may hold values from -0.21875 to 0.21875
Outputs:
- time_core: float32 [768, 512, 3, 128], P('gx', 'gy')
- x_core: float32 [512, 3, 128, 128], P('gy', None, 'gx')
The draws below stay inside these ranges and needn't reach their ends.
All inputs are finite; a program needn't handle non-finite values.
Results may differ from the reference program's by a relative error of at most 0.0003.
Values sent between devices are 32-bit elements; how exact they have to be, the bound alone decides.
A program may use at most 128 MiB of HBM per device.

```python
import math
import jax
import jax.numpy as jnp
from jax import lax

COMP = 3
STEPS = 512
RANK_T = 128
RANK_X = 128
POWER = 3
NX = 768
NY = 512


def draw_motion(key, part):
    key_rough = jax.random.fold_in(key, 11)
    key_wave = jax.random.fold_in(key, 12)
    xpos = jnp.arange(NX, dtype=jnp.float32) / NX
    ypos = jnp.arange(NY, dtype=jnp.float32) / NY
    trend = jnp.exp(0.5 * math.log(3.0) * (xpos[:, None] + ypos[None, :]))
    rough = jnp.exp(jax.random.uniform(key_rough, (NX, NY), jnp.float32, math.log(0.5), math.log(2.0)))
    amp = trend * rough
    comp_index = jnp.arange(COMP, dtype=jnp.float32)
    comp_scale = 1.0 - 0.4 * (comp_index == COMP - 1).astype(jnp.float32)
    wave = jax.random.normal(key_wave, (NX, NY, COMP, STEPS), jnp.float32)
    values = amp[:, :, None, None] * comp_scale[None, None, :, None] * wave
    return jnp.clip(values, -40.0, 40.0)


def scatter_about(stream_key, extent, width, bound, kind=jnp.bfloat16):
    result = jax.random.normal(stream_key, extent, jnp.float32) * width
    return jnp.minimum(jnp.maximum(result, -bound), bound).astype(kind)


def setup_inputs(seed: int = 0) -> dict:
    keys = jax.random.split(jax.random.key(seed), 4)
    motion = draw_motion(jax.random.fold_in(keys[3], 71), 0)
    time_sketch = scatter_about(keys[1], (STEPS, RANK_T), STEPS ** -0.5, 0.25, jnp.float32)
    x_sketch = scatter_about(keys[2], (NX, RANK_X), NX ** -0.5, 0.21875, jnp.float32)
    return {"motion": motion, "time_sketch": time_sketch, "x_sketch": x_sketch}


HIGH = lax.Precision.HIGHEST

def orthonormal(mat):
    gram = jnp.dot(mat.T.astype(jnp.float32), mat.astype(jnp.float32), precision=HIGH, preferred_element_type=jnp.float32)
    lower = jnp.linalg.cholesky(gram)
    return jax.scipy.linalg.solve_triangular(lower, mat.T, lower=True).T

def leading_basis(gram, sketch):
    basis = orthonormal(jnp.dot(gram.astype(jnp.float32), sketch.astype(jnp.float32), precision=HIGH, preferred_element_type=jnp.float32))
    for step in range(POWER - 1):
        basis = orthonormal(jnp.dot(gram.astype(jnp.float32), basis.astype(jnp.float32), precision=HIGH, preferred_element_type=jnp.float32))
    return basis

def reference(motion, time_sketch, x_sketch):
    flat = motion.reshape(NX * NY * COMP, STEPS)
    time_gram = lax.dot_general(flat.astype(jnp.float32), flat.astype(jnp.float32), (((0,), (0,)), ((), ())), precision=HIGH, preferred_element_type=jnp.float32) / (NX * NY * COMP)
    time_basis = leading_basis(time_gram, time_sketch)
    time_core = jnp.dot(flat.astype(jnp.float32), time_basis.astype(jnp.float32), precision=HIGH, preferred_element_type=jnp.float32)
    cols = time_core.reshape(NX, NY * COMP * RANK_T)
    x_gram = jnp.dot(cols.astype(jnp.float32), cols.T.astype(jnp.float32), precision=HIGH, preferred_element_type=jnp.float32) / (NY * COMP * RANK_T)
    x_basis = leading_basis(x_gram, x_sketch)
    x_core = lax.dot_general(cols.astype(jnp.float32), x_basis.astype(jnp.float32), (((0,), (0,)), ((), ())), precision=HIGH, preferred_element_type=jnp.float32)
    return (time_core.reshape(NX, NY, COMP, RANK_T), x_core.reshape(NY, COMP, RANK_T, RANK_X))
```

```python
import functools

import jax
import jax.numpy as jnp
from jax import lax
from jax.experimental import pallas as pl
from jax.experimental.pallas import tpu as pltpu
from jax.sharding import PartitionSpec as P

POWER = 3
HIGH = lax.Precision.HIGHEST
F32 = jnp.float32
BF16 = jnp.bfloat16
MESH = pl.DeviceIdType.MESH
BLK = 256
LANES = 128
N_CORE = 2
N_Y = 4
N_Z = 8
N_X = 4
VMEM = pltpu.VMEM
DMA = pltpu.SemaphoreType.DMA


def upper_blocks(n):
    m = n // BLK
    return [(a, b) for a in range(m) for b in range(a, m)]


def packed_rows(n):
    return len(upper_blocks(n)) * BLK * BLK // LANES


def split(value):
    high = value.astype(BF16)
    low = (value - high.astype(F32)).astype(BF16)
    return high, low


def dot_tn(a, b):
    return lax.dot_general(a, b, (((0,), (0,)), ((), ())), preferred_element_type=F32)


def dot_nt(a, b):
    return lax.dot_general(a, b, (((1,), (1,)), ((), ())), preferred_element_type=F32)


def dot_nn(a, b):
    return lax.dot_general(a, b, (((1,), (0,)), ((), ())), preferred_element_type=F32)


def store_packed(out_ref, index, block):
    for half in range(BLK // LANES):
        row = (index * (BLK // LANES) + half) * BLK
        out_ref[row : row + BLK, :] = block[:, half * LANES : (half + 1) * LANES]


def time_gram_kernel(scale, sizes, unit, m_hbm, out_ref, buf, main_acc, cross_acc, sems):
    n = buf.shape[1]
    blocks = upper_blocks(n)
    loads = []
    for k in range(buf.shape[0] // unit):
        rows = slice(k * unit, (k + 1) * unit)
        loads.append(pltpu.make_async_copy(m_hbm.at[rows], buf.at[rows], sems.at[k]))
        loads[-1].start()
    done = 0
    for size in sizes:
        for load in loads[done : done + size]:
            load.wait()
        high, low = split(buf[done * unit : (done + size) * unit, :])
        for index, (a, b) in enumerate(blocks):
            ca, cb = slice(a * BLK, (a + 1) * BLK), slice(b * BLK, (b + 1) * BLK)
            main = dot_tn(high[:, ca], high[:, cb])
            cross = dot_tn(high[:, ca], low[:, cb])
            if a != b:
                main = main + cross + dot_tn(low[:, ca], high[:, cb])
            if done == 0:
                main_acc[index] = main
                if a == b:
                    cross_acc[a] = cross
            else:
                main_acc[index] += main
                if a == b:
                    cross_acc[a] += cross
        done += size
    for index, (a, b) in enumerate(blocks):
        total = main_acc[index]
        if a == b:
            total = total + cross_acc[a] + cross_acc[a].T
        store_packed(out_ref, index, total * scale)


def time_gram(flat, scale):
    rows, n = flat.shape
    unit = 512
    sizes = (1, 2, 3, 3)
    packed = packed_rows(n)
    return pl.pallas_call(
        functools.partial(time_gram_kernel, scale, sizes, unit),
        out_shape=jax.ShapeDtypeStruct((packed, LANES), F32),
        in_specs=[pl.BlockSpec(memory_space=pl.ANY)],
        out_specs=pl.BlockSpec(memory_space=VMEM),
        scratch_shapes=[
            VMEM((rows, n), F32),
            VMEM((len(upper_blocks(n)), BLK, BLK), F32),
            VMEM((n // BLK, BLK, BLK), F32),
            DMA((rows // unit,)),
        ],
        compiler_params=pltpu.CompilerParams(vmem_limit_bytes=56 << 20),
        name="time_gram",
    )(flat)


def all_reduce_kernel(x_ref, o_ref, r1, a1, r2, a2, r3, a3, r4, send, recv):
    total = x_ref.shape[0]
    half, part, piece = total // N_CORE, total // (N_CORE * N_Y), total // (N_CORE * N_Y * N_Z)
    gx, gy = lax.axis_index("gx"), lax.axis_index("gy")
    core, y = lax.rem(gx, N_CORE), gx // N_CORE
    z, x = lax.rem(gy, N_Z), gy // N_Z

    def at_core():
        return {"gx": y * N_CORE + (1 - core), "gy": gy}

    def at_y(d):
        return {"gx": lax.rem(y + d, N_Y) * N_CORE + core, "gy": gy}

    def at_z(d):
        return {"gx": gx, "gy": x * N_Z + lax.rem(z + d, N_Z)}

    def at_x(d):
        return {"gx": gx, "gy": lax.rem(x + d, N_X) * N_Z + z}

    partners = [at_core()]
    partners += [at_y(d) for d in range(1, N_Y)]
    partners += [at_z(d) for d in range(1, N_Z)]
    partners += [at_x(d) for d in range(1, N_X)]
    barrier = pltpu.get_barrier_semaphore()
    for partner in partners:
        pl.semaphore_signal(barrier, inc=1, device_id=partner, device_id_type=MESH)
    pl.semaphore_wait(barrier, len(partners))

    def rows(start, size):
        return pl.ds(pl.multiple_of(start, 8), size)

    copies = []

    def copy(src, dst, device, number):
        c = pltpu.make_async_remote_copy(
            src_ref=src, dst_ref=dst, send_sem=send.at[number], recv_sem=recv.at[number],
            device_id=device, device_id_type=MESH,
        )
        c.start()
        copies.append(c)
        return c

    number = 0
    order = [1, 2, 3, 0]
    first = []
    for d in order:
        block = lax.rem(y + d, N_Y) * part
        first.append(copy(x_ref.at[rows((1 - core) * half + block, part)], r1.at[rows(block, part)], at_core(), number))
        number += 1
    second = []
    for i, d in enumerate(order):
        block = lax.rem(y + d, N_Y) * part
        first[i].wait_recv()
        a1[rows(block, part), :] = x_ref[rows(core * half + block, part), :] + r1[rows(block, part), :]
        if d:
            second.append(copy(a1.at[rows(block, part)], r2.at[d - 1], at_y(d), number))
            number += 1
    for c in second:
        c.wait_recv()
    a2[...] = a1[rows(y * part, part), :] + r2[0] + r2[1] + r2[2]
    third = []
    for d in range(1, N_Z):
        third.append(copy(a2.at[rows(lax.rem(z + d, N_Z) * piece, piece)], r3.at[d - 1], at_z(d), number))
        number += 1
    for c in third:
        c.wait_recv()
    value = a2[rows(z * piece, piece), :]
    for d in range(1, N_Z):
        value = value + r3[d - 1]
    a3[...] = value
    fourth = []
    for d in range(1, N_X):
        fourth.append(copy(a3, r4.at[x], at_x(d), number))
        number += 1
    r4[x] = value
    for c in fourth:
        c.wait_recv()
    base = core * half + y * part
    mine = rows(base + z * piece, piece)
    o_ref[mine, :] = r4[0] + r4[1] + r4[2] + r4[3]
    fifth = []
    for d in range(1, N_Z):
        fifth.append(copy(o_ref.at[mine], o_ref.at[mine], at_z(d), number))
        number += 1
    for c in fifth:
        c.wait_recv()
    block = rows(base, part)
    sixth = []
    for d in range(1, N_Y):
        sixth.append(copy(o_ref.at[block], o_ref.at[block], at_y(d), number))
        number += 1
    last = [copy(o_ref.at[block], o_ref.at[block], at_core(), number)]
    number += 1
    for d in range(1, N_Y):
        sixth[d - 1].wait_recv()
        other = rows(core * half + lax.rem(y + N_Y - d, N_Y) * part, part)
        last.append(copy(o_ref.at[other], o_ref.at[other], at_core(), number))
        number += 1
    for c in last:
        c.wait_recv()
    for c in copies:
        c.wait_send()


def all_reduce(packed, collective_id):
    total = packed.shape[0]
    half, part, piece = total // N_CORE, total // (N_CORE * N_Y), total // (N_CORE * N_Y * N_Z)
    n = 2 * N_Y + 2 * (N_Y - 1) + 2 * (N_Z - 1) + N_X - 1
    return pl.pallas_call(
        all_reduce_kernel,
        out_shape=jax.ShapeDtypeStruct(packed.shape, F32),
        in_specs=[pl.BlockSpec(memory_space=VMEM)],
        out_specs=pl.BlockSpec(memory_space=VMEM),
        scratch_shapes=[
            VMEM((half, LANES), F32), VMEM((half, LANES), F32),
            VMEM((N_Y - 1, part, LANES), F32), VMEM((part, LANES), F32),
            VMEM((N_Z - 1, piece, LANES), F32), VMEM((piece, LANES), F32),
            VMEM((N_X, piece, LANES), F32),
            DMA((n,)), DMA((n,)),
        ],
        compiler_params=pltpu.CompilerParams(
            collective_id=collective_id, has_side_effects=True, vmem_limit_bytes=32 << 20
        ),
        name="all_reduce_%d" % collective_id,
    )(packed)


def unpack(packed_ref, gram_ref):
    n = gram_ref.shape[0]
    for index, (a, b) in enumerate(upper_blocks(n)):
        for half in range(BLK // LANES):
            row = (index * (BLK // LANES) + half) * BLK
            block = packed_ref[row : row + BLK, :]
            rows = slice(a * BLK, (a + 1) * BLK)
            cols = slice(b * BLK + half * LANES, b * BLK + (half + 1) * LANES)
            gram_ref[rows, cols] = block
            if a != b:
                gram_ref[cols, rows] = block.T


def inverse_cholesky(gram):
    size = gram.shape[0]
    tiles = size // 8
    mat = [gram[8 * t : 8 * t + 8, :] for t in range(tiles)]
    row_id = lax.broadcasted_iota(jnp.int32, (8, size), 0)
    lane_id = lax.broadcasted_iota(jnp.int32, (8, size), 1)
    inv = [jnp.where(lane_id == row_id + 8 * t, 1.0, 0.0).astype(F32) for t in range(tiles)]
    scale = [jnp.zeros((8, size), F32) for t in range(tiles)]
    for k in range(size):
        t, s = k // 8, k % 8
        row = jnp.broadcast_to(mat[t][s : s + 1, :], (8, size))
        row_inv = jnp.broadcast_to(inv[t][s : s + 1, :], (8, size))
        pivot = jnp.broadcast_to(row[:, k : k + 1], (8, size))
        recip = 1.0 / pivot
        scale[t] = jnp.where(row_id == s, lax.rsqrt(pivot), scale[t])
        row_n = row * recip
        row_inv_n = row_inv * recip
        for u in range(t, tiles):
            col = jnp.broadcast_to(mat[u][:, k : k + 1], (8, size))
            if u == t:
                if s == 7:
                    continue
                col = jnp.where(row_id > s, col, 0.0)
            mat[u] = mat[u] - col * row_n
            inv[u] = inv[u] - col * row_inv_n
    return jnp.concatenate([inv[t] * scale[t] for t in range(tiles)], axis=0)


def dot_f32(a, b, dims):
    return lax.dot_general(a, b, (dims, ((), ())), precision=HIGH, preferred_element_type=F32)


def iterate(gram_ref, sketch_ref, basis_ref):
    basis_ref[...] = sketch_ref[...]

    def step(_, carry):
        z = dot_f32(gram_ref[...], basis_ref[...], ((1,), (0,)))
        inv = inverse_cholesky(dot_f32(z, z, ((0,), (0,))))
        basis_ref[...] = dot_f32(z, inv, ((1,), (1,)))
        return carry

    lax.fori_loop(0, POWER, step, 0)


def time_basis_kernel(packed_ref, sketch_ref, basis_ref, gram_ref):
    unpack(packed_ref, gram_ref)
    iterate(gram_ref, sketch_ref, basis_ref)


def time_basis_call(packed, sketch):
    n = sketch.shape[0]
    return pl.pallas_call(
        time_basis_kernel,
        out_shape=jax.ShapeDtypeStruct(sketch.shape, F32),
        in_specs=[pl.BlockSpec(memory_space=VMEM)] * 2,
        out_specs=pl.BlockSpec(memory_space=VMEM),
        scratch_shapes=[VMEM((n, n), F32)],
        compiler_params=pltpu.CompilerParams(vmem_limit_bytes=32 << 20),
        name="time_basis",
    )(packed, sketch)


def project_kernel(scale, n_gx, m_ref, basis_ref, core_ref, cols_hbm, gram_out,
                   basis_h, basis_l, flat, send_buf, cols, gram, send, recv, local):
    c = pl.program_id(0)
    nx, _, ny, steps = m_ref.shape
    ranks = basis_ref.shape[1]
    share = ranks // n_gx
    width = ny * share
    full = nx * n_gx
    me = lax.axis_index("gx")

    @pl.when(c == 0)
    def _():
        barrier = pltpu.get_barrier_semaphore()
        for d in range(1, n_gx):
            pl.semaphore_signal(barrier, inc=1, device_id={"gx": lax.rem(me + d, n_gx)}, device_id_type=MESH)
        high, low = split(basis_ref[...])
        basis_h[...] = high
        basis_l[...] = low
        pl.semaphore_wait(barrier, n_gx - 1)

    high, low = split(m_ref[...].reshape(nx * ny, steps))
    value = dot_nn(high, basis_h[...]) + dot_nn(high, basis_l[...]) + dot_nn(low, basis_h[...])
    flat[...] = value
    core_ref[...] = value.reshape(nx, 1, ny, ranks)

    lane = lax.broadcasted_iota(jnp.int32, (8, LANES), 1) // share
    here = pl.ds(pl.multiple_of(c * width, LANES), width)

    def rearrange(xt, carry):
        for hi in range(ny // 8):
            tiles = [flat[pl.ds(xt * (8 * ny) + hi * 8 + j, 8, stride=ny), :] for j in range(8)]
            for bit in (1, 2, 4):
                keep = (lane & bit) == 0
                for i in range(8):
                    if i & bit:
                        continue
                    a, b = tiles[i], tiles[i | bit]
                    tiles[i] = jnp.where(keep, a, pltpu.roll(b, bit * share, 1))
                    tiles[i | bit] = jnp.where(keep, pltpu.roll(a, LANES - bit * share, 1), b)
            column = pl.ds(pl.multiple_of(c * width + hi * LANES, LANES), LANES)
            for g in range(8):
                send_buf[g, pl.ds(pl.multiple_of(xt * 8, 8), 8), column] = tiles[g]
        return carry

    lax.fori_loop(0, nx // 8, rearrange, 0)
    mine = pl.ds(pl.multiple_of(me * nx, 8), nx)

    def outgoing(d, chunk, columns):
        target = lax.rem(me + d, n_gx)
        return pltpu.make_async_remote_copy(
            src_ref=send_buf.at[target, :, columns], dst_ref=cols.at[mine, columns],
            send_sem=send.at[d - 1, chunk], recv_sem=recv.at[d - 1, chunk],
            device_id={"gx": target}, device_id_type=MESH,
        )

    for d in range(1, n_gx):
        outgoing(d, c, here).start()
    cols[mine, here] = send_buf[me, :, here]

    @pl.when(c == pl.num_programs(0) - 1)
    def _():
        n = full
        blocks = upper_blocks(n)
        stores = []
        for chunk in range(cols.shape[1] // width):
            columns = slice(chunk * width, (chunk + 1) * width)
            for d in range(1, n_gx):
                outgoing(d, chunk, columns).wait_recv()
            stores.append(pltpu.make_async_copy(cols.at[:, columns], cols_hbm.at[:, columns], local.at[chunk]))
            stores[-1].start()
            high, low = split(cols[:, columns])
            for index, (a, b) in enumerate(blocks):
                ra, rb = slice(a * BLK, (a + 1) * BLK), slice(b * BLK, (b + 1) * BLK)
                cross = dot_nt(high[ra], low[rb])
                cross = cross + (cross.T if a == b else dot_nt(low[ra], high[rb]))
                block = dot_nt(high[ra], high[rb]) + cross
                if chunk == 0:
                    gram[index] = block
                else:
                    gram[index] += block
        for index in range(len(blocks)):
            store_packed(gram_out, index, gram[index] * scale)
        for copy in stores:
            copy.wait()
        for chunk in range(cols.shape[1] // width):
            for d in range(1, n_gx):
                outgoing(d, chunk, slice(chunk * width, (chunk + 1) * width)).wait_send()


def project(motion, basis, scale, n_gx):
    nx, comps, ny, steps = motion.shape
    ranks = basis.shape[1]
    share = ranks // n_gx
    width = ny * share
    full = nx * n_gx
    packed = packed_rows(full)
    n_blocks = len(upper_blocks(full))
    return pl.pallas_call(
        functools.partial(project_kernel, scale, n_gx),
        out_shape=(
            jax.ShapeDtypeStruct((nx, comps, ny, ranks), F32),
            jax.ShapeDtypeStruct((full, comps * width), F32),
            jax.ShapeDtypeStruct((packed, LANES), F32),
        ),
        grid=(comps,),
        in_specs=[
            pl.BlockSpec((nx, 1, ny, steps), lambda c: (0, c, 0, 0)),
            pl.BlockSpec((steps, ranks), lambda c: (0, 0)),
        ],
        out_specs=(
            pl.BlockSpec((nx, 1, ny, ranks), lambda c: (0, c, 0, 0)),
            pl.BlockSpec(memory_space=pl.ANY),
            pl.BlockSpec((packed, LANES), lambda c: (0, 0)),
        ),
        scratch_shapes=[
            VMEM((steps, ranks), BF16), VMEM((steps, ranks), BF16),
            VMEM((nx * ny, ranks), F32),
            VMEM((n_gx, nx, comps * width), F32),
            VMEM((full, comps * width), F32),
            VMEM((n_blocks, BLK, BLK), F32),
            DMA((n_gx - 1, comps)), DMA((n_gx - 1, comps)), DMA((comps,)),
        ],
        compiler_params=pltpu.CompilerParams(
            collective_id=2, has_side_effects=True, vmem_limit_bytes=56 << 20
        ),
        name="project",
    )(motion, basis)


def x_kernel(comps, packed_ref, sketch_ref, cols_hbm, core_hbm, out_ref, core_out, gram_ref, basis_ref, cols, sems):
    load = pltpu.make_async_copy(cols_hbm, cols, sems.at[0])
    move = pltpu.make_async_copy(core_hbm, core_out, sems.at[1])
    load.start()
    move.start()
    unpack(packed_ref, gram_ref)
    iterate(gram_ref, sketch_ref, basis_ref)
    load.wait()
    ny, _, share, _ = out_ref.shape
    width = ny * share
    bh, bl = split(basis_ref[...])
    for c in range(comps):
        high, low = split(cols[:, c * width : (c + 1) * width])
        value = dot_tn(high, bh) + dot_tn(high, bl) + dot_tn(low, bh)
        for y in range(ny):
            out_ref[y, c] = value[y * share : (y + 1) * share, :]
    move.wait()


def x_call(packed, sketch, cols, core, share):
    n, ranks = sketch.shape
    nx, comps, ny, _ = core.shape
    return pl.pallas_call(
        functools.partial(x_kernel, comps),
        out_shape=(
            jax.ShapeDtypeStruct((ny, comps, share, ranks), F32),
            jax.ShapeDtypeStruct(core.shape, F32),
        ),
        in_specs=[
            pl.BlockSpec(memory_space=VMEM), pl.BlockSpec(memory_space=VMEM),
            pl.BlockSpec(memory_space=pl.ANY), pl.BlockSpec(memory_space=pl.ANY),
        ],
        out_specs=(pl.BlockSpec(memory_space=VMEM), pl.BlockSpec(memory_space=pl.ANY)),
        scratch_shapes=[VMEM((n, n), F32), VMEM((n, ranks), F32), VMEM(cols.shape, F32), DMA((2,))],
        compiler_params=pltpu.CompilerParams(vmem_limit_bytes=40 << 20),
        name="x_basis",
    )(packed, sketch, cols, core)


def shards(n_gx, n_gy, motion, time_sketch, x_sketch):
    nx, ny, comps, steps = motion.shape
    ranks = time_sketch.shape[1]
    ordered = motion.transpose(0, 2, 1, 3)
    sites = nx * n_gx * ny * n_gy * comps
    packed = time_gram(ordered.reshape(nx * comps * ny, steps), 1.0 / sites)
    basis = time_basis_call(all_reduce(packed, 0), time_sketch)
    core, cols, packed = project(ordered, basis, 1.0 / (ny * n_gy * comps * ranks), n_gx)
    x_core, core = x_call(all_reduce(packed, 1), x_sketch, cols, core, ranks // n_gx)
    return core.transpose(0, 2, 1, 3), x_core


def solution(mesh):
    in_specs = (P("gx", "gy", None, None), P(), P())
    out_specs = (P("gx", "gy", None, None), P("gy", None, "gx", None))
    return jax.shard_map(
        functools.partial(shards, mesh.shape["gx"], mesh.shape["gy"]),
        mesh=mesh, in_specs=in_specs, out_specs=out_specs, check_vma=False,
    )
```

```python
import functools

import jax
import jax.numpy as jnp
from jax import lax
from jax.experimental import pallas as pl
from jax.experimental.pallas import tpu as pltpu
from jax.sharding import PartitionSpec as P

POWER = 3
HIGH = lax.Precision.HIGHEST
F32 = jnp.float32
BF16 = jnp.bfloat16
MESH = pl.DeviceIdType.MESH
BLK = 256
LANES = 128
N_CORE = 2
N_Y = 4
N_Z = 8
N_X = 4
VMEM = pltpu.VMEM
DMA = pltpu.SemaphoreType.DMA


def upper_blocks(n):
    m = n // BLK
    return [(a, b) for a in range(m) for b in range(a, m)]


def packed_rows(n):
    return len(upper_blocks(n)) * BLK * BLK // LANES


def split(value):
    high = value.astype(BF16)
    low = (value - high.astype(F32)).astype(BF16)
    return high, low


def dot_tn(a, b):
    return lax.dot_general(a, b, (((0,), (0,)), ((), ())), preferred_element_type=F32)


def dot_nt(a, b):
    return lax.dot_general(a, b, (((1,), (1,)), ((), ())), preferred_element_type=F32)


def dot_nn(a, b):
    return lax.dot_general(a, b, (((1,), (0,)), ((), ())), preferred_element_type=F32)


def store_packed(out_ref, index, block):
    for half in range(BLK // LANES):
        row = (index * (BLK // LANES) + half) * BLK
        out_ref[row : row + BLK, :] = block[:, half * LANES : (half + 1) * LANES]


def time_gram_kernel(scale, sizes, unit, m_hbm, out_ref, buf, main_acc, cross_acc, sems):
    n = buf.shape[1]
    blocks = upper_blocks(n)
    loads = []
    for k in range(buf.shape[0] // unit):
        rows = slice(k * unit, (k + 1) * unit)
        loads.append(pltpu.make_async_copy(m_hbm.at[rows], buf.at[rows], sems.at[k]))
        loads[-1].start()
    done = 0
    for size in sizes:
        for load in loads[done : done + size]:
            load.wait()
        high, low = split(buf[done * unit : (done + size) * unit, :])
        for index, (a, b) in enumerate(blocks):
            ca, cb = slice(a * BLK, (a + 1) * BLK), slice(b * BLK, (b + 1) * BLK)
            main = dot_tn(high[:, ca], high[:, cb])
            cross = dot_tn(high[:, ca], low[:, cb])
            if a != b:
                main = main + cross + dot_tn(low[:, ca], high[:, cb])
            if done == 0:
                main_acc[index] = main
                if a == b:
                    cross_acc[a] = cross
            else:
                main_acc[index] += main
                if a == b:
                    cross_acc[a] += cross
        done += size
    for index, (a, b) in enumerate(blocks):
        total = main_acc[index]
        if a == b:
            total = total + cross_acc[a] + cross_acc[a].T
        store_packed(out_ref, index, total * scale)


def time_gram(flat, scale):
    rows, n = flat.shape
    unit = 512
    sizes = (1, 2, 3, 3)
    packed = packed_rows(n)
    return pl.pallas_call(
        functools.partial(time_gram_kernel, scale, sizes, unit),
        out_shape=jax.ShapeDtypeStruct((packed, LANES), F32),
        in_specs=[pl.BlockSpec(memory_space=pl.ANY)],
        out_specs=pl.BlockSpec(memory_space=VMEM),
        scratch_shapes=[
            VMEM((rows, n), F32),
            VMEM((len(upper_blocks(n)), BLK, BLK), F32),
            VMEM((n // BLK, BLK, BLK), F32),
            DMA((rows // unit,)),
        ],
        compiler_params=pltpu.CompilerParams(vmem_limit_bytes=56 << 20),
        name="time_gram",
    )(flat)


def all_reduce_kernel(x_ref, o_ref, r1, a1, r2, a2, r3, a3, r4, send, recv):
    total = x_ref.shape[0]
    half, part, piece = total // N_CORE, total // (N_CORE * N_Y), total // (N_CORE * N_Y * N_Z)
    gx, gy = lax.axis_index("gx"), lax.axis_index("gy")
    core, y = lax.rem(gx, N_CORE), gx // N_CORE
    z, x = lax.rem(gy, N_Z), gy // N_Z

    def at_core():
        return {"gx": y * N_CORE + (1 - core), "gy": gy}

    def at_y(d):
        return {"gx": lax.rem(y + d, N_Y) * N_CORE + core, "gy": gy}

    def at_z(d):
        return {"gx": gx, "gy": x * N_Z + lax.rem(z + d, N_Z)}

    def at_x(d):
        return {"gx": gx, "gy": lax.rem(x + d, N_X) * N_Z + z}

    partners = [at_core()]
    partners += [at_y(d) for d in range(1, N_Y)]
    partners += [at_z(d) for d in range(1, N_Z)]
    partners += [at_x(d) for d in range(1, N_X)]
    barrier = pltpu.get_barrier_semaphore()
    for partner in partners:
        pl.semaphore_signal(barrier, inc=1, device_id=partner, device_id_type=MESH)
    pl.semaphore_wait(barrier, len(partners))

    def rows(start, size):
        return pl.ds(pl.multiple_of(start, 8), size)

    copies = []

    def copy(src, dst, device, number):
        c = pltpu.make_async_remote_copy(
            src_ref=src, dst_ref=dst, send_sem=send.at[number], recv_sem=recv.at[number],
            device_id=device, device_id_type=MESH,
        )
        c.start()
        copies.append(c)
        return c

    number = 0
    order = [1, 2, 3, 0]
    first = []
    for d in order:
        block = lax.rem(y + d, N_Y) * part
        first.append(copy(x_ref.at[rows((1 - core) * half + block, part)], r1.at[rows(block, part)], at_core(), number))
        number += 1
    second = []
    for i, d in enumerate(order):
        block = lax.rem(y + d, N_Y) * part
        first[i].wait_recv()
        a1[rows(block, part), :] = x_ref[rows(core * half + block, part), :] + r1[rows(block, part), :]
        if d:
            second.append(copy(a1.at[rows(block, part)], r2.at[d - 1], at_y(d), number))
            number += 1
    for c in second:
        c.wait_recv()
    a2[...] = a1[rows(y * part, part), :] + r2[0] + r2[1] + r2[2]
    third = []
    for d in range(1, N_Z):
        third.append(copy(a2.at[rows(lax.rem(z + d, N_Z) * piece, piece)], r3.at[d - 1], at_z(d), number))
        number += 1
    for c in third:
        c.wait_recv()
    value = a2[rows(z * piece, piece), :]
    for d in range(1, N_Z):
        value = value + r3[d - 1]
    a3[...] = value
    fourth = []
    for d in range(1, N_X):
        fourth.append(copy(a3, r4.at[x], at_x(d), number))
        number += 1
    r4[x] = value
    for c in fourth:
        c.wait_recv()
    base = core * half + y * part
    mine = rows(base + z * piece, piece)
    o_ref[mine, :] = r4[0] + r4[1] + r4[2] + r4[3]
    fifth = []
    for d in range(1, N_Z):
        fifth.append(copy(o_ref.at[mine], o_ref.at[mine], at_z(d), number))
        number += 1
    for c in fifth:
        c.wait_recv()
    block = rows(base, part)
    sixth = []
    for d in range(1, N_Y):
        sixth.append(copy(o_ref.at[block], o_ref.at[block], at_y(d), number))
        number += 1
    last = [copy(o_ref.at[block], o_ref.at[block], at_core(), number)]
    number += 1
    for d in range(1, N_Y):
        sixth[d - 1].wait_recv()
        other = rows(core * half + lax.rem(y + N_Y - d, N_Y) * part, part)
        last.append(copy(o_ref.at[other], o_ref.at[other], at_core(), number))
        number += 1
    for c in last:
        c.wait_recv()
    for c in copies:
        c.wait_send()


def all_reduce(packed, collective_id):
    total = packed.shape[0]
    half, part, piece = total // N_CORE, total // (N_CORE * N_Y), total // (N_CORE * N_Y * N_Z)
    n = 2 * N_Y + 2 * (N_Y - 1) + 2 * (N_Z - 1) + N_X - 1
    return pl.pallas_call(
        all_reduce_kernel,
        out_shape=jax.ShapeDtypeStruct(packed.shape, F32),
        in_specs=[pl.BlockSpec(memory_space=VMEM)],
        out_specs=pl.BlockSpec(memory_space=VMEM),
        scratch_shapes=[
            VMEM((half, LANES), F32), VMEM((half, LANES), F32),
            VMEM((N_Y - 1, part, LANES), F32), VMEM((part, LANES), F32),
            VMEM((N_Z - 1, piece, LANES), F32), VMEM((piece, LANES), F32),
            VMEM((N_X, piece, LANES), F32),
            DMA((n,)), DMA((n,)),
        ],
        compiler_params=pltpu.CompilerParams(
            collective_id=collective_id, has_side_effects=True, vmem_limit_bytes=32 << 20
        ),
        name="all_reduce_%d" % collective_id,
    )(packed)


def unpack(packed_ref, gram_ref):
    n = gram_ref.shape[0]
    for index, (a, b) in enumerate(upper_blocks(n)):
        for half in range(BLK // LANES):
            row = (index * (BLK // LANES) + half) * BLK
            block = packed_ref[row : row + BLK, :]
            rows = slice(a * BLK, (a + 1) * BLK)
            cols = slice(b * BLK + half * LANES, b * BLK + (half + 1) * LANES)
            gram_ref[rows, cols] = block
            if a != b:
                gram_ref[cols, rows] = block.T


def split3(value):
    high = value.astype(BF16).astype(F32)
    rest = value - high
    mid = rest.astype(BF16).astype(F32)
    return high, mid, rest - mid


def inverse_cholesky(gram):
    size = gram.shape[0]
    tiles = size // 8
    row_id = lax.broadcasted_iota(jnp.int32, (8, size), 0)
    lane_id = lax.broadcasted_iota(jnp.int32, (8, size), 1)
    mat = [gram[8 * t : 8 * t + 8, :] for t in range(tiles)]
    inv = [jnp.where(lane_id == row_id + 8 * t, 1.0, 0.0).astype(F32) for t in range(tiles)]
    is_row = [row_id == i for i in range(8)]
    out = []

    def fill(value):
        return jnp.broadcast_to(value, (8, size))

    pending = None
    for t in range(tiles):
        block = [fill(mat[t][:, 8 * t + j : 8 * t + j + 1]) for j in range(8)]
        s = {(i, j): fill(block[j][i : i + 1, :]) for j in range(8) for i in range(j, 8)}
        rows = [fill(mat[t][i : i + 1, :]) for i in range(8)]
        rows_inv = [fill(inv[t][i : i + 1, :]) for i in range(8)]
        if pending is not None:
            for u in range(t + 1, tiles):
                mat[u] = mat[u] - pending[8 * u : 8 * u + 8, :size]
                inv[u] = inv[u] - pending[8 * u : 8 * u + 8, size:]
        recips, low, v = [], {}, {}
        for m in range(8):
            recip = 1.0 / s[(m, m)]
            recips.append(recip)
            for i in range(m + 1, 8):
                low[(i, m)] = s[(i, m)] * recip
            for j in range(m + 1, 8):
                for i in range(j, 8):
                    s[(i, j)] = s[(i, j)] - low[(i, m)] * s[(j, m)]
            i = m + 1
            if i < 8:
                for j in range(i):
                    total = -low[(i, j)]
                    for q in range(j + 1, i):
                        total = total - low[(i, q)] * v[(q, j)]
                    v[(i, j)] = total
        scale = recips[0]
        for i in range(1, 8):
            scale = jnp.where(is_row[i], recips[i], scale)
        done, done_inv = mat[t], inv[t]
        for j in range(7):
            coef = jnp.zeros((8, size), F32)
            for i in range(j + 1, 8):
                coef = jnp.where(is_row[i], v[(i, j)], coef)
            done = done + coef * rows[j]
            done_inv = done_inv + coef * rows_inv[j]
        out.append(done_inv * jnp.sqrt(scale))
        if t + 1 < tiles:
            cols = [fill(mat[t + 1][:, 8 * t + j : 8 * t + j + 1]) for j in range(8)]
            scaled = []
            for i in range(8):
                total = cols[i]
                for j in range(i):
                    total = total + v[(i, j)] * cols[j]
                scaled.append(total * recips[i])
            for j in range(8):
                weight = scaled[j]
                for i in range(j + 1, 8):
                    weight = weight + scaled[i] * v[(i, j)]
                mat[t + 1] = mat[t + 1] - weight * rows[j]
                inv[t + 1] = inv[t + 1] - weight * rows_inv[j]
        if t + 2 < tiles:
            lh, lm, ll = split3(done * scale)
            rh, rm, rl = split3(jnp.concatenate([done, done_inv], axis=1))
            left = jnp.concatenate([lh, lh, lm, lh, ll, lm], axis=0).astype(BF16)
            right = jnp.concatenate([rh, rm, rh, rl, rh, rm], axis=0).astype(BF16)
            pending = dot_tn(left, right)
    return jnp.concatenate(out, axis=0)


def dot_f32(a, b, dims):
    return lax.dot_general(a, b, (dims, ((), ())), precision=HIGH, preferred_element_type=F32)


def iterate(gram_ref, sketch_ref, basis_ref):
    basis_ref[...] = sketch_ref[...]

    def step(_, carry):
        z = dot_f32(gram_ref[...], basis_ref[...], ((1,), (0,)))
        inv = inverse_cholesky(dot_f32(z, z, ((0,), (0,))))
        basis_ref[...] = dot_f32(z, inv, ((1,), (1,)))
        return carry

    lax.fori_loop(0, POWER, step, 0)


def time_basis_kernel(packed_ref, sketch_ref, basis_ref, gram_ref):
    unpack(packed_ref, gram_ref)
    iterate(gram_ref, sketch_ref, basis_ref)


def time_basis_call(packed, sketch):
    n = sketch.shape[0]
    return pl.pallas_call(
        time_basis_kernel,
        out_shape=jax.ShapeDtypeStruct(sketch.shape, F32),
        in_specs=[pl.BlockSpec(memory_space=VMEM)] * 2,
        out_specs=pl.BlockSpec(memory_space=VMEM),
        scratch_shapes=[VMEM((n, n), F32)],
        compiler_params=pltpu.CompilerParams(vmem_limit_bytes=32 << 20),
        name="time_basis",
    )(packed, sketch)


def project_kernel(scale, n_gx, m_ref, basis_ref, core_ref, cols_hbm, gram_out,
                   basis_h, basis_l, flat, send_buf, cols, gram, send, recv, local):
    c = pl.program_id(0)
    nx, _, ny, steps = m_ref.shape
    ranks = basis_ref.shape[1]
    share = ranks // n_gx
    width = ny * share
    full = nx * n_gx
    me = lax.axis_index("gx")

    @pl.when(c == 0)
    def _():
        barrier = pltpu.get_barrier_semaphore()
        for d in range(1, n_gx):
            pl.semaphore_signal(barrier, inc=1, device_id={"gx": lax.rem(me + d, n_gx)}, device_id_type=MESH)
        high, low = split(basis_ref[...])
        basis_h[...] = high
        basis_l[...] = low
        pl.semaphore_wait(barrier, n_gx - 1)

    high, low = split(m_ref[...].reshape(nx * ny, steps))
    value = dot_nn(high, basis_h[...]) + dot_nn(high, basis_l[...]) + dot_nn(low, basis_h[...])
    flat[...] = value
    core_ref[...] = value.reshape(nx, 1, ny, ranks)

    lane = lax.broadcasted_iota(jnp.int32, (8, LANES), 1) // share
    here = pl.ds(pl.multiple_of(c * width, LANES), width)

    def rearrange(xt, carry):
        for hi in range(ny // 8):
            tiles = [flat[pl.ds(xt * (8 * ny) + hi * 8 + j, 8, stride=ny), :] for j in range(8)]
            for bit in (1, 2, 4):
                keep = (lane & bit) == 0
                for i in range(8):
                    if i & bit:
                        continue
                    a, b = tiles[i], tiles[i | bit]
                    tiles[i] = jnp.where(keep, a, pltpu.roll(b, bit * share, 1))
                    tiles[i | bit] = jnp.where(keep, pltpu.roll(a, LANES - bit * share, 1), b)
            column = pl.ds(pl.multiple_of(c * width + hi * LANES, LANES), LANES)
            for g in range(8):
                send_buf[g, pl.ds(pl.multiple_of(xt * 8, 8), 8), column] = tiles[g]
        return carry

    lax.fori_loop(0, nx // 8, rearrange, 0)
    mine = pl.ds(pl.multiple_of(me * nx, 8), nx)

    def outgoing(d, chunk, columns):
        target = lax.rem(me + d, n_gx)
        return pltpu.make_async_remote_copy(
            src_ref=send_buf.at[target, :, columns], dst_ref=cols.at[mine, columns],
            send_sem=send.at[d - 1, chunk], recv_sem=recv.at[d - 1, chunk],
            device_id={"gx": target}, device_id_type=MESH,
        )

    for d in range(1, n_gx):
        outgoing(d, c, here).start()
    cols[mine, here] = send_buf[me, :, here]

    @pl.when(c == pl.num_programs(0) - 1)
    def _():
        n = full
        blocks = upper_blocks(n)
        stores = []
        for chunk in range(cols.shape[1] // width):
            columns = slice(chunk * width, (chunk + 1) * width)
            for d in range(1, n_gx):
                outgoing(d, chunk, columns).wait_recv()
            stores.append(pltpu.make_async_copy(cols.at[:, columns], cols_hbm.at[:, columns], local.at[chunk]))
            stores[-1].start()
            high, low = split(cols[:, columns])
            for index, (a, b) in enumerate(blocks):
                ra, rb = slice(a * BLK, (a + 1) * BLK), slice(b * BLK, (b + 1) * BLK)
                cross = dot_nt(high[ra], low[rb])
                cross = cross + (cross.T if a == b else dot_nt(low[ra], high[rb]))
                block = dot_nt(high[ra], high[rb]) + cross
                if chunk == 0:
                    gram[index] = block
                else:
                    gram[index] += block
        for index in range(len(blocks)):
            store_packed(gram_out, index, gram[index] * scale)
        for copy in stores:
            copy.wait()
        for chunk in range(cols.shape[1] // width):
            for d in range(1, n_gx):
                outgoing(d, chunk, slice(chunk * width, (chunk + 1) * width)).wait_send()


def project(motion, basis, scale, n_gx):
    nx, comps, ny, steps = motion.shape
    ranks = basis.shape[1]
    share = ranks // n_gx
    width = ny * share
    full = nx * n_gx
    packed = packed_rows(full)
    n_blocks = len(upper_blocks(full))
    return pl.pallas_call(
        functools.partial(project_kernel, scale, n_gx),
        out_shape=(
            jax.ShapeDtypeStruct((nx, comps, ny, ranks), F32),
            jax.ShapeDtypeStruct((full, comps * width), F32),
            jax.ShapeDtypeStruct((packed, LANES), F32),
        ),
        grid=(comps,),
        in_specs=[
            pl.BlockSpec((nx, 1, ny, steps), lambda c: (0, c, 0, 0)),
            pl.BlockSpec((steps, ranks), lambda c: (0, 0)),
        ],
        out_specs=(
            pl.BlockSpec((nx, 1, ny, ranks), lambda c: (0, c, 0, 0)),
            pl.BlockSpec(memory_space=pl.ANY),
            pl.BlockSpec((packed, LANES), lambda c: (0, 0)),
        ),
        scratch_shapes=[
            VMEM((steps, ranks), BF16), VMEM((steps, ranks), BF16),
            VMEM((nx * ny, ranks), F32),
            VMEM((n_gx, nx, comps * width), F32),
            VMEM((full, comps * width), F32),
            VMEM((n_blocks, BLK, BLK), F32),
            DMA((n_gx - 1, comps)), DMA((n_gx - 1, comps)), DMA((comps,)),
        ],
        compiler_params=pltpu.CompilerParams(
            collective_id=2, has_side_effects=True, vmem_limit_bytes=56 << 20
        ),
        name="project",
    )(motion, basis)


def x_kernel(comps, packed_ref, sketch_ref, cols_hbm, core_hbm, out_ref, core_out, gram_ref, basis_ref, cols, sems):
    load = pltpu.make_async_copy(cols_hbm, cols, sems.at[0])
    move = pltpu.make_async_copy(core_hbm, core_out, sems.at[1])
    load.start()
    move.start()
    unpack(packed_ref, gram_ref)
    iterate(gram_ref, sketch_ref, basis_ref)
    load.wait()
    ny, _, share, _ = out_ref.shape
    width = ny * share
    bh, bl = split(basis_ref[...])
    for c in range(comps):
        high, low = split(cols[:, c * width : (c + 1) * width])
        value = dot_tn(high, bh) + dot_tn(high, bl) + dot_tn(low, bh)
        for y in range(ny):
            out_ref[y, c] = value[y * share : (y + 1) * share, :]
    move.wait()


def x_call(packed, sketch, cols, core, share):
    n, ranks = sketch.shape
    nx, comps, ny, _ = core.shape
    return pl.pallas_call(
        functools.partial(x_kernel, comps),
        out_shape=(
            jax.ShapeDtypeStruct((ny, comps, share, ranks), F32),
            jax.ShapeDtypeStruct(core.shape, F32),
        ),
        in_specs=[
            pl.BlockSpec(memory_space=VMEM), pl.BlockSpec(memory_space=VMEM),
            pl.BlockSpec(memory_space=pl.ANY), pl.BlockSpec(memory_space=pl.ANY),
        ],
        out_specs=(pl.BlockSpec(memory_space=VMEM), pl.BlockSpec(memory_space=pl.ANY)),
        scratch_shapes=[VMEM((n, n), F32), VMEM((n, ranks), F32), VMEM(cols.shape, F32), DMA((2,))],
        compiler_params=pltpu.CompilerParams(vmem_limit_bytes=40 << 20),
        name="x_basis",
    )(packed, sketch, cols, core)


def shards(n_gx, n_gy, motion, time_sketch, x_sketch):
    nx, ny, comps, steps = motion.shape
    ranks = time_sketch.shape[1]
    ordered = motion.transpose(0, 2, 1, 3)
    sites = nx * n_gx * ny * n_gy * comps
    packed = time_gram(ordered.reshape(nx * comps * ny, steps), 1.0 / sites)
    basis = time_basis_call(all_reduce(packed, 0), time_sketch)
    core, cols, packed = project(ordered, basis, 1.0 / (ny * n_gy * comps * ranks), n_gx)
    x_core, core = x_call(all_reduce(packed, 1), x_sketch, cols, core, ranks // n_gx)
    return core.transpose(0, 2, 1, 3), x_core


def solution(mesh):
    in_specs = (P("gx", "gy", None, None), P(), P())
    out_specs = (P("gx", "gy", None, None), P("gy", None, "gx", None))
    return jax.shard_map(
        functools.partial(shards, mesh.shape["gx"], mesh.shape["gy"]),
        mesh=mesh, in_specs=in_specs, out_specs=out_specs, check_vma=False,
    )
```
